128 devices in a mesh: grp: 8 (over y, core), seq: 16 (over z, x).
Axes of the slice: x: 4, y: 4, z: 4, core: 2. Of those that a mesh axis runs over, the one named last changes fastest.
Arguments:
- queries: bfloat16 [131072, 1024], P(('grp', 'seq')), may hold values from -6 to 6
- key_rows: bfloat16 [131072, 1024], P(('grp', 'seq')), may hold values from -6 to 6
- value_rows: bfloat16 [131072, 1024], P(('grp', 'seq')), may hold values from -6 to 6
- norm_gain: float32 [1024], replicated, may hold values from 0.25 to 1.75
- cotangent: bfloat16 [131072, 1024], P(('grp', 'seq')), may hold values from -6 to 6
Outputs:
- normed_out: bfloat16 [131072, 1024], P(('grp', 'seq'))
- grad_queries: bfloat16 [131072, 1024], P(('grp', 'seq'))
- grad_keys: bfloat16 [131072, 1024], P(('grp', 'seq'))
- grad_values: bfloat16 [131072, 1024], P(('grp', 'seq'))
The draws below stay inside these ranges and needn't reach their ends.
All inputs are finite; a program needn't handle non-finite values.
Results may differ from the reference program's by a relative error of at most 0.0058.
Values sent between devices are 32-bit elements; how exact they have to be, the bound alone decides.
A program may use at most 128 MiB of HBM per device.

```python
import jax
import jax.numpy as jnp
from jax import lax

H = 8
HD = 128
BLOCK = 512
D = 1024
TOKENS = 131072


def levels(own_key, shape, pieces, least, largest):
    factor_of = 1.0
    for position, parts in pieces:
        draws = jax.random.uniform(jax.random.fold_in(jax.random.fold_in(own_key, 6), position), (parts,), jnp.float32, least / len(pieces), largest / len(pieces))
        factor_of = factor_of * jnp.repeat(jnp.exp(draws), shape[position] // parts).reshape((-1,) + (1,) * (len(shape) - 1 - position))
    return factor_of


def noise(key, dims, spread, reach, pieces=(), kind=jnp.bfloat16):
    drawn = jax.random.normal(key, dims, jnp.float32) * spread
    if len(pieces) > 0:
        drawn = levels(key, dims, pieces, -0.22, 0.18) * drawn
    return jnp.clip(drawn, min=-reach, max=reach).astype(kind)


def setup_inputs(seed: int = 0) -> dict:
    splits = jax.random.split(jax.random.key(seed), 6)
    queries = noise(splits[0], (TOKENS, D), 1.0, 6.0, ((0, 128),))
    key_rows = noise(splits[1], (TOKENS, D), 1.0, 6.0, ((0, 128),))
    value_rows = noise(splits[2], (TOKENS, D), 1.0, 6.0, ((0, 128),))
    norm_gain = jnp.clip(1.0 + 0.15 * jax.random.normal(splits[3], (D,), jnp.float32), 0.25, 1.75)
    cotangent = noise(splits[4], (TOKENS, D), 1.0, 6.0, ((0, 128),))
    return {"queries": queries, "key_rows": key_rows, "value_rows": value_rows, "norm_gain": norm_gain, "cotangent": cotangent}


EPSILON = 1e-06

def lower_mask(length):
    indices = jnp.arange(length)
    return indices[:, None] >= indices[None, :]

def round_half(value):
    return lax.optimization_barrier(value.astype(jnp.bfloat16)).astype(jnp.float32)

def reference(queries, key_rows, value_rows, norm_gain, cotangent):
    block_count = TOKENS // BLOCK
    features = H * HD
    block_shape = (block_count, BLOCK, H, HD)
    query_blocks = queries.reshape(block_shape)
    key_blocks = key_rows.reshape(block_shape)
    value_blocks = value_rows.reshape(block_shape)
    causal = lower_mask(BLOCK)[None]
    zero_state = jnp.zeros((H, HD, HD), jnp.float32)

    def forward_step(carry_state, inputs):
        query_blk, key_blk, value_blk = [member.astype(jnp.float32) for member in inputs]
        prior_state = round_half(carry_state)
        scores = jnp.einsum('thd,shd->hts', query_blk, key_blk)
        scores = round_half(jnp.where(causal, scores, 0.0))
        mixed_rows = jnp.einsum('hts,she->the', scores, value_blk)
        mixed_rows = mixed_rows + jnp.einsum('thd,hde->the', query_blk, prior_state)
        carry_state = carry_state + jnp.einsum('shd,she->hde', key_blk, value_blk)
        return (carry_state, (mixed_rows, prior_state))
    final_state, (attended, priors) = lax.scan(forward_step, zero_state, (query_blocks, key_blocks, value_blocks))
    attended = attended.reshape(TOKENS, features)
    inverse = lax.rsqrt(lax.optimization_barrier(jnp.mean(attended * attended, axis=1, keepdims=True)) + EPSILON)
    unit_rows = attended * inverse
    gain_rows = norm_gain.astype(jnp.float32)[None, :]
    normed_out = (unit_rows * gain_rows).astype(jnp.bfloat16)
    scaled = cotangent.astype(jnp.float32) * gain_rows
    grad_attended = inverse * (scaled - unit_rows * lax.optimization_barrier(jnp.mean(scaled * unit_rows, axis=1, keepdims=True)))
    grad_blocks = grad_attended.astype(jnp.bfloat16).reshape(block_shape)

    def backward_step(carry_state, inputs):
        query_blk, key_blk, value_blk, grad_blk = [member.astype(jnp.float32) for member in inputs[:4]]
        prior_state = inputs[4]
        later_state = round_half(carry_state)
        scores = jnp.einsum('thd,shd->hts', query_blk, key_blk)
        scores = round_half(jnp.where(causal, scores, 0.0))
        grad_scores = jnp.einsum('the,she->hts', grad_blk, value_blk)
        grad_scores = round_half(jnp.where(causal, grad_scores, 0.0))
        grad_q = jnp.einsum('hts,shd->thd', grad_scores, key_blk) + jnp.einsum('the,hde->thd', grad_blk, prior_state)
        grad_k = jnp.einsum('hts,thd->shd', grad_scores, query_blk) + jnp.einsum('she,hde->shd', value_blk, later_state)
        grad_v = jnp.einsum('hts,the->she', scores, grad_blk) + jnp.einsum('shd,hde->she', key_blk, later_state)
        carry_state = carry_state + jnp.einsum('thd,the->hde', query_blk, grad_blk)
        return (carry_state, (grad_q.astype(jnp.bfloat16), grad_k.astype(jnp.bfloat16), grad_v.astype(jnp.bfloat16)))
    final_grad, (grad_q, grad_k, grad_v) = lax.scan(backward_step, zero_state, (query_blocks, key_blocks, value_blocks, grad_blocks, priors), reverse=True)
    return (normed_out, grad_q.reshape(TOKENS, features), grad_k.reshape(TOKENS, features), grad_v.reshape(TOKENS, features))
```

```python
import functools

import jax
import jax.numpy as jnp
from jax import lax
from jax.experimental import pallas as pl
from jax.experimental.pallas import tpu as pltpu
from jax.sharding import PartitionSpec as P

H = 8
HD = 128
BLOCK = 512
HALF = 256
D = H * HD
TOK = 1024
CHUNKS = 2
HPC = H // CHUNKS
EPSILON = 1e-06
F32 = jnp.float32
BF16 = jnp.bfloat16
MESH = pl.DeviceIdType.MESH


def dot_nn(a, b):
    return lax.dot_general(a, b, (((1,), (0,)), ((), ())), preferred_element_type=F32)


def dot_nt(a, b):
    return lax.dot_general(a, b, (((1,), (1,)), ((), ())), preferred_element_type=F32)


def dot_tn(a, b):
    return lax.dot_general(a, b, (((0,), (0,)), ((), ())), preferred_element_type=F32)


def causal(tile):
    rows = lax.broadcasted_iota(jnp.int32, tile.shape, 0)
    cols = lax.broadcasted_iota(jnp.int32, tile.shape, 1)
    return jnp.where(rows >= cols, tile, 0.0)


def kernel(
    groups, shards,
    q_hbm, k_hbm, v_hbm, gain_ref, dy_hbm,
    no_hbm, gq_hbm, gk_hbm, gv_hbm,
    qh, kh, vh, dyh, sc, att, ga, lk, lv, no_s, gq_s, gk_s, gv_s,
    own, arrived, before, total, peers, result, inner, prior,
    squares, dots, inv_rows, mix_rows,
    in_sem, out_sem, send_sem, recv_sem,
):
    grp = lax.axis_index("grp")
    seq = lax.axis_index("seq")
    sub = HPC * HD // shards
    per_head = HD // sub

    def columns(h):
        return pl.ds(pl.multiple_of(h * HD, HD), HD)

    def load(i, h):
        src = (k_hbm, v_hbm, q_hbm, dy_hbm)[i]
        dst = (kh, vh, qh, dyh)[i]
        return pltpu.make_async_copy(src.at[:, columns(h)], dst.at[h], in_sem.at[i, h])

    def store(i, h):
        src = (no_s, gq_s, gk_s, gv_s)[i]
        dst = (no_hbm, gq_hbm, gk_hbm, gv_hbm)[i]
        return pltpu.make_async_copy(src.at[h], dst.at[:, columns(h)], out_sem.at[i, h])

    def each(lo, hi, fn):
        def step(h, carry):
            fn(h)
            return carry
        lax.fori_loop(lo, hi, step, 0)

    def start_loads(arrays):
        def one(h):
            for i in arrays:
                load(i, h).start()
        each(0, H, one)

    def send_parts(w, c):
        def one(d):
            to = lax.rem(seq + d, shards)
            pltpu.make_async_remote_copy(
                own.at[w, c, to], arrived.at[w, c, seq],
                send_sem.at[w, c, 0], recv_sem.at[w, c, 0],
                device_id=(grp, to), device_id_type=MESH,
            ).start()
        each(1, shards, one)
        arrived[w, c, seq] = own[w, c, seq]

    def wait_parts(w, c):
        pltpu.make_async_remote_copy(
            own.at[w, c, pl.ds(0, shards - 1)], arrived.at[w, c, pl.ds(0, shards - 1)],
            send_sem.at[w, c, 0], recv_sem.at[w, c, 0],
            device_id=(grp, seq), device_id_type=MESH,
        ).wait_recv()

    def scan_parts(w, c):
        wait_parts(w, c)
        order = range(shards) if w == 0 else range(shards - 1, -1, -1)
        running = jnp.zeros((sub, HD), F32)
        for t in order:
            before[w, c, t] = running
            running = running + arrived[w, c, t]
        total[w, c] = running

        def one(d):
            to = lax.rem(grp + d, groups)
            pltpu.make_async_remote_copy(
                total.at[w, c], peers.at[w, c, grp],
                send_sem.at[w, c, 1], recv_sem.at[w, c, 1],
                device_id=(to, seq), device_id_type=MESH,
            ).start()
        each(1, groups, one)

    def return_parts(w, c):
        pltpu.make_async_remote_copy(
            peers.at[w, c, pl.ds(0, groups - 1)], peers.at[w, c, pl.ds(0, groups - 1)],
            send_sem.at[w, c, 1], recv_sem.at[w, c, 1],
            device_id=(grp, seq), device_id_type=MESH,
        ).wait_recv()
        lo, hi = (0, grp) if w == 0 else (grp + 1, groups)
        base = lax.fori_loop(
            lo, hi, lambda g, s: s + peers[w, c, g], jnp.zeros((sub, HD), F32)
        )
        for t in range(shards):
            before[w, c, t] = before[w, c, t] + base

        def one(d):
            to = lax.rem(seq + d, shards)
            pltpu.make_async_remote_copy(
                before.at[w, c, to], result.at[w, c, seq],
                send_sem.at[w, c, 2], recv_sem.at[w, c, 2],
                device_id=(grp, to), device_id_type=MESH,
            ).start()
        each(1, shards, one)
        result[w, c, seq] = before[w, c, seq]

    def wait_result(w, c):
        pltpu.make_async_remote_copy(
            before.at[w, c, pl.ds(0, shards - 1)], result.at[w, c, pl.ds(0, shards - 1)],
            send_sem.at[w, c, 2], recv_sem.at[w, c, 2],
            device_id=(grp, seq), device_id_type=MESH,
        ).wait_recv()

    def wait_sends(w, c):
        for phase, ref, count in ((0, own, shards), (1, peers, groups), (2, before, shards)):
            pltpu.make_async_remote_copy(
                ref.at[w, c, pl.ds(0, count - 1)], ref.at[w, c, pl.ds(0, count - 1)],
                send_sem.at[w, c, phase], recv_sem.at[w, c, phase],
                device_id=(grp, seq), device_id_type=MESH,
            ).wait_send()

    def put_own(w, h, value):
        c = h // HPC
        at = pl.multiple_of((h % HPC) * per_head, per_head)
        own[w, c, pl.ds(at, per_head)] = value.reshape(per_head, sub, HD)

    def get_result(w, h):
        c = h // HPC
        at = pl.multiple_of((h % HPC) * per_head, per_head)
        return result[w, c, pl.ds(at, per_head)].reshape(HD, HD)

    def first(b, i):
        return pl.ds(b * BLOCK + i * HALF, HALF)

    def block(b):
        return pl.ds(b * BLOCK, BLOCK)

    def key_state(h):
        load(0, h).wait()
        load(1, h).wait()
        s0 = dot_tn(kh[h, block(0)], vh[h, block(0)])
        s1 = dot_tn(kh[h, block(1)], vh[h, block(1)])
        inner[0, h] = s0
        put_own(0, h, s0 + s1)

    def local(h):
        for b in range(2):
            q0, q1 = qh[h, first(b, 0)], qh[h, first(b, 1)]
            k0, k1 = kh[h, first(b, 0)], kh[h, first(b, 1)]
            v0, v1 = vh[h, first(b, 0)], vh[h, first(b, 1)]
            t00 = causal(dot_nt(q0, k0)).astype(BF16)
            t10 = dot_nt(q1, k0).astype(BF16)
            t11 = causal(dot_nt(q1, k1)).astype(BF16)
            sc[h, b, 0] = t00
            sc[h, b, 1] = t10
            sc[h, b, 2] = t11
            att[h, first(b, 0)] = dot_nn(t00, v0)
            att[h, first(b, 1)] = dot_nn(t10, v0) + dot_nn(t11, v1)

    def attend(h):
        base = get_result(0, h)
        states = (base.astype(BF16), (base + inner[0, h]).astype(BF16))
        gain = gain_ref[h]
        for b in range(2):
            prior[h, b] = states[b]
            for i in range(2):
                rows = first(b, i)
                value = att[h, rows] + dot_nn(qh[h, rows], states[b])
                att[h, rows] = value
                scaled = dyh[h, rows].astype(F32) * gain
                squares[rows] = squares[rows] + value * value
                dots[rows] = dots[rows] + scaled * value

    def row_factors():
        for b in range(2):
            for i in range(2):
                rows = first(b, i)
                mean_sq = jnp.sum(squares[rows], axis=1, keepdims=True) * (1.0 / D)
                mean_dot = jnp.sum(dots[rows], axis=1, keepdims=True) * (1.0 / D)
                inverse = lax.rsqrt(mean_sq + EPSILON)
                mix = inverse * inverse * (inverse * mean_dot)
                inv_rows[rows] = jnp.broadcast_to(inverse, (HALF, HD))
                mix_rows[rows] = jnp.broadcast_to(mix, (HALF, HD))

    def grad_state(h):
        gain = gain_ref[h]
        parts = []
        for b in range(2):
            rows = block(b)
            scaled = dyh[h, rows].astype(F32) * gain
            grad = (inv_rows[rows] * scaled - mix_rows[rows] * att[h, rows]).astype(BF16)
            ga[h, rows] = grad
            parts.append(dot_tn(qh[h, rows], grad))
        inner[1, h] = parts[1]
        put_own(1, h, parts[0] + parts[1])

    def normed(h):
        gain = gain_ref[h]
        no_s[h] = (att[h] * inv_rows[...] * gain).astype(BF16)
        store(0, h).start()

    def backward(h):
        normed(h)
        for b in range(2):
            q0, q1 = qh[h, first(b, 0)], qh[h, first(b, 1)]
            k0, k1 = kh[h, first(b, 0)], kh[h, first(b, 1)]
            v0, v1 = vh[h, first(b, 0)], vh[h, first(b, 1)]
            g0, g1 = ga[h, first(b, 0)], ga[h, first(b, 1)]
            p = prior[h, b]
            s00 = causal(dot_nt(g0, v0)).astype(BF16)
            s10 = dot_nt(g1, v0).astype(BF16)
            s11 = causal(dot_nt(g1, v1)).astype(BF16)
            gq_s[h, first(b, 0)] = (dot_nt(g0, p) + dot_nn(s00, k0)).astype(BF16)
            gq_s[h, first(b, 1)] = (dot_nt(g1, p) + dot_nn(s10, k0) + dot_nn(s11, k1)).astype(BF16)
            lk[h, first(b, 0)] = dot_tn(s00, q0) + dot_tn(s10, q1)
            lk[h, first(b, 1)] = dot_tn(s11, q1)
            lv[h, first(b, 0)] = dot_tn(sc[h, b, 0], g0) + dot_tn(sc[h, b, 1], g1)
            lv[h, first(b, 1)] = dot_tn(sc[h, b, 2], g1)
        store(1, h).start()

    def finish(h):
        base = get_result(1, h)
        states = ((base + inner[1, h]).astype(BF16), base.astype(BF16))
        for b in range(2):
            rows = block(b)
            gk_s[h, rows] = (lk[h, rows] + dot_nt(vh[h, rows], states[b])).astype(BF16)
            gv_s[h, rows] = (lv[h, rows] + dot_nn(kh[h, rows], states[b])).astype(BF16)
        store(2, h).start()
        store(3, h).start()

    start_loads((0, 1))
    barrier = pltpu.get_barrier_semaphore()

    def greet_seq(d):
        pl.semaphore_signal(
            barrier, inc=1, device_id=(grp, lax.rem(seq + d, shards)), device_id_type=MESH
        )

    def greet_grp(d):
        pl.semaphore_signal(
            barrier, inc=1, device_id=(lax.rem(grp + d, groups), seq), device_id_type=MESH
        )

    each(1, shards, greet_seq)
    each(1, groups, greet_grp)
    start_loads((2, 3))

    each(0, HPC, key_state)
    pl.semaphore_wait(barrier, shards - 1 + groups - 1)
    send_parts(0, 0)
    each(HPC, H, key_state)
    send_parts(0, 1)

    def wait_q(h):
        load(2, h).wait()
        load(3, h).wait()

    each(0, H, wait_q)
    squares[...] = jnp.zeros_like(squares)
    dots[...] = jnp.zeros_like(dots)
    each(0, 4, local)
    scan_parts(0, 0)
    each(4, 6, local)
    scan_parts(0, 1)
    return_parts(0, 0)
    each(6, 8, local)
    return_parts(0, 1)
    wait_result(0, 0)
    each(0, HPC, attend)
    wait_result(0, 1)
    each(HPC, H, attend)
    row_factors()
    each(0, HPC, grad_state)
    send_parts(1, 0)
    each(HPC, H, grad_state)
    send_parts(1, 1)
    each(0, 3, backward)
    scan_parts(1, 0)
    each(3, 5, backward)
    scan_parts(1, 1)
    return_parts(1, 0)
    each(5, 8, backward)
    return_parts(1, 1)
    wait_result(1, 0)
    each(0, HPC, finish)
    wait_result(1, 1)
    each(HPC, H, finish)
    for w in range(2):
        for c in range(CHUNKS):
            wait_sends(w, c)

    def wait_stores(h):
        for i in range(4):
            store(i, h).wait()

    each(0, H, wait_stores)


def body(groups, shards, queries, key_rows, value_rows, norm_gain, cotangent):
    sub = HPC * HD // shards
    whole = jax.ShapeDtypeStruct((TOK, D), BF16)
    anywhere = pl.BlockSpec(memory_space=pl.ANY)
    heads = lambda kind: pltpu.VMEM((H, TOK, HD), kind)
    parts = pltpu.VMEM((2, CHUNKS, shards, sub, HD), F32)
    return tuple(pl.pallas_call(
        functools.partial(kernel, groups, shards),
        out_shape=(whole,) * 4,
        in_specs=[anywhere, anywhere, anywhere, pl.BlockSpec(memory_space=pltpu.VMEM), anywhere],
        out_specs=(anywhere,) * 4,
        scratch_shapes=[
            heads(BF16), heads(BF16), heads(BF16), heads(BF16),
            pltpu.VMEM((H, 2, 3, HALF, HALF), BF16),
            heads(F32), heads(BF16), heads(F32), heads(F32),
            heads(BF16), heads(BF16), heads(BF16), heads(BF16),
            parts, parts, parts,
            pltpu.VMEM((2, CHUNKS, sub, HD), F32),
            pltpu.VMEM((2, CHUNKS, groups, sub, HD), F32),
            parts,
            pltpu.VMEM((2, H, HD, HD), F32),
            pltpu.VMEM((H, 2, HD, HD), BF16),
            pltpu.VMEM((TOK, HD), F32), pltpu.VMEM((TOK, HD), F32),
            pltpu.VMEM((TOK, HD), F32), pltpu.VMEM((TOK, HD), F32),
            pltpu.SemaphoreType.DMA((4, H)),
            pltpu.SemaphoreType.DMA((4, H)),
            pltpu.SemaphoreType.DMA((2, CHUNKS, 3)),
            pltpu.SemaphoreType.DMA((2, CHUNKS, 3)),
        ],
        compiler_params=pltpu.CompilerParams(
            collective_id=0, has_side_effects=True, vmem_limit_bytes=60 * 1024 * 1024
        ),
        name="attention",
    )(queries, key_rows, value_rows, norm_gain.reshape(H, 1, HD), cotangent))


def solution(mesh):
    rows = P(("grp", "seq"), None)
    return jax.shard_map(
        functools.partial(body, mesh.shape["grp"], mesh.shape["seq"]),
        mesh=mesh,
        in_specs=(rows, rows, rows, P(), rows),
        out_specs=(rows,) * 4,
        check_vma=False,
    )
```

```python
import functools

import jax
import jax.numpy as jnp
from jax import lax
from jax.experimental import pallas as pl
from jax.experimental.pallas import tpu as pltpu
from jax.sharding import PartitionSpec as P

H = 8
HD = 128
BLOCK = 512
HALF = 256
D = H * HD
TOK = 1024
CHUNKS = 4
HPC = H // CHUNKS
EPSILON = 1e-06
F32 = jnp.float32
BF16 = jnp.bfloat16
MESH = pl.DeviceIdType.MESH


def dot_nn(a, b):
    return lax.dot_general(a, b, (((1,), (0,)), ((), ())), preferred_element_type=F32)


def dot_nt(a, b):
    return lax.dot_general(a, b, (((1,), (1,)), ((), ())), preferred_element_type=F32)


def dot_tn(a, b):
    return lax.dot_general(a, b, (((0,), (0,)), ((), ())), preferred_element_type=F32)


def causal(tile):
    rows = lax.broadcasted_iota(jnp.int32, tile.shape, 0)
    cols = lax.broadcasted_iota(jnp.int32, tile.shape, 1)
    return jnp.where(rows >= cols, tile, 0.0)


def kernel(
    groups, shards,
    q_hbm, k_hbm, v_hbm, gain_hbm, dy_hbm,
    no_ref, gq_ref, gk_ref, gv_ref,
    qh, kh, vh, dyh, sc, att, ga, lk, lv,
    own, arrived, before, total, peers, result, inner, prior,
    squares, dots, inv_rows, mix_rows,
    gain_ref, in_sem, gain_sem, send_sem, recv_sem,
):
    grp = lax.axis_index("grp")
    seq = lax.axis_index("seq")
    sub = HPC * HD // shards
    per_head = HD // sub

    def columns(h):
        return pl.ds(pl.multiple_of(h * HD, HD), HD)

    def load(i, h):
        src = (k_hbm, v_hbm, q_hbm, dy_hbm)[i]
        dst = (kh, vh, qh, dyh)[i]
        return pltpu.make_async_copy(src.at[:, columns(h)], dst.at[h], in_sem.at[i, h])

    def each(lo, hi, fn):
        def step(h, carry):
            fn(h)
            return carry
        lax.fori_loop(lo, hi, step, 0)

    def start_loads(arrays):
        def one(h):
            for i in arrays:
                load(i, h).start()
        each(0, H, one)

    def send_parts(w, c):
        def one(d):
            to = lax.rem(seq + d, shards)
            pltpu.make_async_remote_copy(
                own.at[w, c, to], arrived.at[w, c, seq],
                send_sem.at[w, c, 0], recv_sem.at[w, c, 0],
                device_id=(grp, to), device_id_type=MESH,
            ).start()
        each(1, shards, one)
        arrived[w, c, seq] = own[w, c, seq]

    def wait_parts(w, c):
        pltpu.make_async_remote_copy(
            own.at[w, c, pl.ds(0, shards - 1)], arrived.at[w, c, pl.ds(0, shards - 1)],
            send_sem.at[w, c, 0], recv_sem.at[w, c, 0],
            device_id=(grp, seq), device_id_type=MESH,
        ).wait_recv()

    def scan_parts(w, c):
        wait_parts(w, c)
        order = range(shards) if w == 0 else range(shards - 1, -1, -1)
        running = jnp.zeros((sub, HD), F32)
        for t in order:
            before[w, c, t] = running
            running = running + arrived[w, c, t]
        total[w, c] = running

        def one(d):
            to = lax.rem(grp + d, groups)
            pltpu.make_async_remote_copy(
                total.at[w, c], peers.at[w, c, grp],
                send_sem.at[w, c, 1], recv_sem.at[w, c, 1],
                device_id=(to, seq), device_id_type=MESH,
            ).start()
        each(1, groups, one)

    def return_parts(w, c):
        pltpu.make_async_remote_copy(
            peers.at[w, c, pl.ds(0, groups - 1)], peers.at[w, c, pl.ds(0, groups - 1)],
            send_sem.at[w, c, 1], recv_sem.at[w, c, 1],
            device_id=(grp, seq), device_id_type=MESH,
        ).wait_recv()
        lo, hi = (0, grp) if w == 0 else (grp + 1, groups)
        base = lax.fori_loop(
            lo, hi, lambda g, s: s + peers[w, c, g], jnp.zeros((sub, HD), F32)
        )
        for t in range(shards):
            before[w, c, t] = before[w, c, t] + base

        def one(d):
            to = lax.rem(seq + d, shards)
            pltpu.make_async_remote_copy(
                before.at[w, c, to], result.at[w, c, seq],
                send_sem.at[w, c, 2], recv_sem.at[w, c, 2],
                device_id=(grp, to), device_id_type=MESH,
            ).start()
        each(1, shards, one)
        result[w, c, seq] = before[w, c, seq]

    def wait_result(w, c):
        pltpu.make_async_remote_copy(
            before.at[w, c, pl.ds(0, shards - 1)], result.at[w, c, pl.ds(0, shards - 1)],
            send_sem.at[w, c, 2], recv_sem.at[w, c, 2],
            device_id=(grp, seq), device_id_type=MESH,
        ).wait_recv()

    def wait_sends(w, c):
        for phase, ref, count in ((0, own, shards), (1, peers, groups), (2, before, shards)):
            pltpu.make_async_remote_copy(
                ref.at[w, c, pl.ds(0, count - 1)], ref.at[w, c, pl.ds(0, count - 1)],
                send_sem.at[w, c, phase], recv_sem.at[w, c, phase],
                device_id=(grp, seq), device_id_type=MESH,
            ).wait_send()

    def put_own(w, h, value):
        c = h // HPC
        at = pl.multiple_of((h % HPC) * per_head, per_head)
        own[w, c, pl.ds(at, per_head)] = value.reshape(per_head, sub, HD)

    def get_result(w, h):
        c = h // HPC
        at = pl.multiple_of((h % HPC) * per_head, per_head)
        return result[w, c, pl.ds(at, per_head)].reshape(HD, HD)

    def first(b, i):
        return pl.ds(b * BLOCK + i * HALF, HALF)

    def block(b):
        return pl.ds(b * BLOCK, BLOCK)

    def key_state(h):
        load(0, h).wait()
        load(1, h).wait()
        s0 = dot_tn(kh[h, block(0)], vh[h, block(0)])
        s1 = dot_tn(kh[h, block(1)], vh[h, block(1)])
        inner[0, h] = s0
        put_own(0, h, s0 + s1)

    def local(h):
        for b in range(2):
            q0, q1 = qh[h, first(b, 0)], qh[h, first(b, 1)]
            k0, k1 = kh[h, first(b, 0)], kh[h, first(b, 1)]
            v0, v1 = vh[h, first(b, 0)], vh[h, first(b, 1)]
            t00 = causal(dot_nt(q0, k0)).astype(BF16)
            t10 = dot_nt(q1, k0).astype(BF16)
            t11 = causal(dot_nt(q1, k1)).astype(BF16)
            sc[h, b, 0] = t00
            sc[h, b, 1] = t10
            sc[h, b, 2] = t11
            att[h, first(b, 0)] = dot_nn(t00, v0)
            att[h, first(b, 1)] = dot_nn(t10, v0) + dot_nn(t11, v1)

    def attend(h):
        base = get_result(0, h)
        states = (base.astype(BF16), (base + inner[0, h]).astype(BF16))
        gain = gain_ref[h]
        for b in range(2):
            prior[h, b] = states[b]
            for i in range(2):
                rows = first(b, i)
                value = att[h, rows] + dot_nn(qh[h, rows], states[b])
                att[h, rows] = value
                scaled = dyh[h, rows].astype(F32) * gain
                squares[rows] = squares[rows] + value * value
                dots[rows] = dots[rows] + scaled * value

    def row_factors():
        for b in range(2):
            for i in range(2):
                rows = first(b, i)
                mean_sq = jnp.sum(squares[rows], axis=1, keepdims=True) * (1.0 / D)
                mean_dot = jnp.sum(dots[rows], axis=1, keepdims=True) * (1.0 / D)
                inverse = lax.rsqrt(mean_sq + EPSILON)
                mix = inverse * inverse * (inverse * mean_dot)
                inv_rows[rows] = jnp.broadcast_to(inverse, (HALF, HD))
                mix_rows[rows] = jnp.broadcast_to(mix, (HALF, HD))

    def grad_state(h):
        gain = gain_ref[h]
        parts = []
        for b in range(2):
            rows = block(b)
            scaled = dyh[h, rows].astype(F32) * gain
            grad = (inv_rows[rows] * scaled - mix_rows[rows] * att[h, rows]).astype(BF16)
            ga[h, rows] = grad
            parts.append(dot_tn(qh[h, rows], grad))
        inner[1, h] = parts[1]
        put_own(1, h, parts[0] + parts[1])

    def normed(h):
        gain = gain_ref[h]
        no_ref[:, columns(h)] = (att[h] * inv_rows[...] * gain).astype(BF16)

    def backward(h):
        normed(h)
        for b in range(2):
            q0, q1 = qh[h, first(b, 0)], qh[h, first(b, 1)]
            k0, k1 = kh[h, first(b, 0)], kh[h, first(b, 1)]
            v0, v1 = vh[h, first(b, 0)], vh[h, first(b, 1)]
            g0, g1 = ga[h, first(b, 0)], ga[h, first(b, 1)]
            p = prior[h, b]
            s00 = causal(dot_nt(g0, v0)).astype(BF16)
            s10 = dot_nt(g1, v0).astype(BF16)
            s11 = causal(dot_nt(g1, v1)).astype(BF16)
            gq_ref[first(b, 0), columns(h)] = (dot_nt(g0, p) + dot_nn(s00, k0)).astype(BF16)
            gq_ref[first(b, 1), columns(h)] = (dot_nt(g1, p) + dot_nn(s10, k0) + dot_nn(s11, k1)).astype(BF16)
            lk[h, first(b, 0)] = dot_tn(s00, q0) + dot_tn(s10, q1)
            lk[h, first(b, 1)] = dot_tn(s11, q1)
            lv[h, first(b, 0)] = dot_tn(sc[h, b, 0], g0) + dot_tn(sc[h, b, 1], g1)
            lv[h, first(b, 1)] = dot_tn(sc[h, b, 2], g1)

    def finish(h):
        base = get_result(1, h)
        states = ((base + inner[1, h]).astype(BF16), base.astype(BF16))
        for b in range(2):
            rows = block(b)
            gk_ref[rows, columns(h)] = (lk[h, rows] + dot_nt(vh[h, rows], states[b])).astype(BF16)
            gv_ref[rows, columns(h)] = (lv[h, rows] + dot_nn(kh[h, rows], states[b])).astype(BF16)

    barrier = pltpu.get_barrier_semaphore()

    def greet_seq(d):
        pl.semaphore_signal(
            barrier, inc=1, device_id=(grp, lax.rem(seq + d, shards)), device_id_type=MESH
        )

    def greet_grp(d):
        pl.semaphore_signal(
            barrier, inc=1, device_id=(lax.rem(grp + d, groups), seq), device_id_type=MESH
        )

    each(1, shards, greet_seq)
    each(1, groups, greet_grp)
    start_loads((0, 1))
    start_loads((2, 3))
    gain_copy = pltpu.make_async_copy(gain_hbm, gain_ref, gain_sem)
    gain_copy.start()

    for c in range(CHUNKS):
        each(c * HPC, (c + 1) * HPC, key_state)
        if c == 0:
            pl.semaphore_wait(barrier, shards - 1 + groups - 1)
        send_parts(0, c)

    def wait_q(h):
        load(2, h).wait()
        load(3, h).wait()

    each(0, H, wait_q)
    gain_copy.wait()
    squares[...] = jnp.zeros_like(squares)
    dots[...] = jnp.zeros_like(dots)
    each(0, 6, local)
    scan_parts(0, 0)
    each(6, 7, local)
    scan_parts(0, 1)
    each(7, 8, local)
    scan_parts(0, 2)
    return_parts(0, 0)
    scan_parts(0, 3)
    return_parts(0, 1)
    return_parts(0, 2)
    return_parts(0, 3)
    for c in range(CHUNKS):
        wait_result(0, c)
        each(c * HPC, (c + 1) * HPC, attend)
    row_factors()
    for c in range(CHUNKS):
        each(c * HPC, (c + 1) * HPC, grad_state)
        send_parts(1, c)
    each(0, 3, backward)
    scan_parts(1, 0)
    each(3, 4, backward)
    scan_parts(1, 1)
    each(4, 5, backward)
    scan_parts(1, 2)
    return_parts(1, 0)
    each(5, 6, backward)
    scan_parts(1, 3)
    return_parts(1, 1)
    return_parts(1, 2)
    return_parts(1, 3)
    each(6, 8, backward)
    for c in range(CHUNKS):
        wait_result(1, c)
        each(c * HPC, (c + 1) * HPC, finish)
    for w in range(2):
        for c in range(CHUNKS):
            wait_sends(w, c)


def body(groups, shards, queries, key_rows, value_rows, norm_gain, cotangent):
    sub = HPC * HD // shards
    whole = pltpu.VMEM((TOK, D), BF16)
    anywhere = pl.BlockSpec(memory_space=pltpu.HBM)
    heads = lambda kind: pltpu.VMEM((H, TOK, HD), kind)
    parts = pltpu.VMEM((2, CHUNKS, shards, sub, HD), F32)
    return tuple(pl.pallas_call(
        functools.partial(kernel, groups, shards),
        out_shape=(whole,) * 4,
        in_specs=[anywhere] * 5,
        out_specs=(pl.BlockSpec(memory_space=pltpu.VMEM),) * 4,
        scratch_shapes=[
            heads(BF16), heads(BF16), heads(BF16), heads(BF16),
            pltpu.VMEM((H, 2, 3, HALF, HALF), BF16),
            heads(F32), heads(BF16), heads(F32), heads(F32),
            parts, parts, parts,
            pltpu.VMEM((2, CHUNKS, sub, HD), F32),
            pltpu.VMEM((2, CHUNKS, groups, sub, HD), F32),
            parts,
            pltpu.VMEM((2, H, HD, HD), F32),
            pltpu.VMEM((H, 2, HD, HD), BF16),
            pltpu.VMEM((TOK, HD), F32), pltpu.VMEM((TOK, HD), F32),
            pltpu.VMEM((TOK, HD), F32), pltpu.VMEM((TOK, HD), F32),
            pltpu.VMEM((H, 1, HD), F32),
            pltpu.SemaphoreType.DMA((4, H)),
            pltpu.SemaphoreType.DMA,
            pltpu.SemaphoreType.DMA((2, CHUNKS, 3)),
            pltpu.SemaphoreType.DMA((2, CHUNKS, 3)),
        ],
        compiler_params=pltpu.CompilerParams(
            collective_id=0, has_side_effects=True, vmem_limit_bytes=40 * 1024 * 1024
        ),
        name="attention",
    )(queries, key_rows, value_rows, norm_gain.reshape(H, 1, HD), cotangent))


def solution(mesh):
    rows = P(("grp", "seq"), None)
    return jax.shard_map(
        functools.partial(body, mesh.shape["grp"], mesh.shape["seq"]),
        mesh=mesh,
        in_specs=(rows, rows, rows, P(), rows),
        out_specs=(rows,) * 4,
        check_vma=False,
    )
```

```python
import functools

import jax
import jax.numpy as jnp
from jax import lax
from jax.experimental import pallas as pl
from jax.experimental.pallas import tpu as pltpu
from jax.sharding import PartitionSpec as P

H = 8
HD = 128
BLOCK = 512
HALF = 256
D = H * HD
TOK = 1024
CHUNKS = 4
HPC = H // CHUNKS
PIECES = 2
EPSILON = 1e-06
F32 = jnp.float32
BF16 = jnp.bfloat16
MESH = pl.DeviceIdType.MESH


def dot_nn(a, b):
    return lax.dot_general(a, b, (((1,), (0,)), ((), ())), preferred_element_type=F32)


def dot_nt(a, b):
    return lax.dot_general(a, b, (((1,), (1,)), ((), ())), preferred_element_type=F32)


def dot_tn(a, b):
    return lax.dot_general(a, b, (((0,), (0,)), ((), ())), preferred_element_type=F32)


def causal(tile):
    rows = lax.broadcasted_iota(jnp.int32, tile.shape, 0)
    cols = lax.broadcasted_iota(jnp.int32, tile.shape, 1)
    return jnp.where(rows >= cols, tile, 0.0)


def kernel(
    groups, shards,
    q_hbm, k_hbm, v_hbm, gain_hbm, dy_hbm,
    no_ref, gq_ref, gk_ref, gv_ref,
    qh, kh, vh, dyh, sc, att, ga, lk, lv,
    own, arrived, before, total, peers, result, inner, prior,
    squares, dots, inv_rows, mix_rows,
    gain_ref, in_sem, gain_sem, send_sem, recv_sem,
):
    grp = lax.axis_index("grp")
    seq = lax.axis_index("seq")
    sub = HPC * HD // shards
    per_head = HD // sub

    def ring(step):
        return min(step, 4 - step)

    offsets = [(dz, dx) for dz in range(shards // 4) for dx in range(4) if dz or dx]
    offsets.sort(key=lambda o: -ring(o[0]) - ring(o[1]))
    shard_peers = [
        lax.rem(seq // 4 + dz, shards // 4) * 4 + lax.rem(seq % 4 + dx, 4) for dz, dx in offsets
    ]
    offsets = [(dy, dc) for dy in range(groups // 2) for dc in range(2) if dy or dc]
    offsets.sort(key=lambda o: -ring(o[0]) * 2 - o[1])
    group_peers = [
        lax.rem(grp // 2 + dy, groups // 2) * 2 + lax.rem(grp % 2 + dc, 2) for dy, dc in offsets
    ]

    def columns(h):
        return pl.ds(pl.multiple_of(h * HD, HD), HD)

    def load(i, h):
        src = (k_hbm, v_hbm, q_hbm, dy_hbm)[i]
        dst = (kh, vh, qh, dyh)[i]
        return pltpu.make_async_copy(src.at[:, columns(h)], dst.at[h], in_sem.at[i, h])

    def each(lo, hi, fn):
        def step(h, carry):
            fn(h)
            return carry
        lax.fori_loop(lo, hi, step, 0)

    def start_loads(arrays):
        def one(h):
            for i in arrays:
                load(i, h).start()
        each(0, H, one)

    def send_parts(w, c):
        for to in shard_peers:
            pltpu.make_async_remote_copy(
                own.at[w, c, to], arrived.at[w, c, seq],
                send_sem.at[w, c, 0], recv_sem.at[w, c, 0],
                device_id=(grp, to), device_id_type=MESH,
            ).start()
        arrived[w, c, seq] = own[w, c, seq]

    def wait_parts(w, c):
        pltpu.make_async_remote_copy(
            own.at[w, c, pl.ds(0, shards - 1)], arrived.at[w, c, pl.ds(0, shards - 1)],
            send_sem.at[w, c, 0], recv_sem.at[w, c, 0],
            device_id=(grp, seq), device_id_type=MESH,
        ).wait_recv()

    def scan_parts(w, c):
        wait_parts(w, c)
        order = range(shards) if w == 0 else range(shards - 1, -1, -1)
        running = jnp.zeros((sub, HD), F32)
        for t in order:
            before[w, c, t] = running
            running = running + arrived[w, c, t]
        total[w, c] = running

        for to in group_peers:
            pltpu.make_async_remote_copy(
                total.at[w, c], peers.at[w, c, grp],
                send_sem.at[w, c, 1], recv_sem.at[w, c, 1],
                device_id=(to, seq), device_id_type=MESH,
            ).start()

    def return_parts(w, c):
        pltpu.make_async_remote_copy(
            peers.at[w, c, pl.ds(0, groups - 1)], peers.at[w, c, pl.ds(0, groups - 1)],
            send_sem.at[w, c, 1], recv_sem.at[w, c, 1],
            device_id=(grp, seq), device_id_type=MESH,
        ).wait_recv()
        lo, hi = (0, grp) if w == 0 else (grp + 1, groups)
        base = lax.fori_loop(
            lo, hi, lambda g, s: s + peers[w, c, g], jnp.zeros((sub, HD), F32)
        )
        for t in range(shards):
            before[w, c, t] = before[w, c, t] + base

        for to in shard_peers:
            pltpu.make_async_remote_copy(
                before.at[w, c, to], result.at[w, c, seq],
                send_sem.at[w, c, 2], recv_sem.at[w, c, 2],
                device_id=(grp, to), device_id_type=MESH,
            ).start()
        result[w, c, seq] = before[w, c, seq]

    def wait_result(w, c):
        pltpu.make_async_remote_copy(
            before.at[w, c, pl.ds(0, shards - 1)], result.at[w, c, pl.ds(0, shards - 1)],
            send_sem.at[w, c, 2], recv_sem.at[w, c, 2],
            device_id=(grp, seq), device_id_type=MESH,
        ).wait_recv()

    def wait_sends(w, c):
        for phase, ref, count in ((0, own, shards), (1, peers, groups), (2, before, shards)):
            pltpu.make_async_remote_copy(
                ref.at[w, c, pl.ds(0, count - 1)], ref.at[w, c, pl.ds(0, count - 1)],
                send_sem.at[w, c, phase], recv_sem.at[w, c, phase],
                device_id=(grp, seq), device_id_type=MESH,
            ).wait_send()

    def put_own(w, h, value):
        c = h // HPC
        at = pl.multiple_of((h % HPC) * per_head, per_head)
        own[w, c, pl.ds(at, per_head)] = value.reshape(per_head, sub, HD)

    def get_result(w, h):
        c = h // HPC
        at = pl.multiple_of((h % HPC) * per_head, per_head)
        return result[w, c, pl.ds(at, per_head)].reshape(HD, HD)

    def first(b, i):
        return pl.ds(b * BLOCK + i * HALF, HALF)

    def block(b):
        return pl.ds(b * BLOCK, BLOCK)

    def key_state(h):
        load(0, h).wait()
        load(1, h).wait()
        s0 = dot_tn(kh[h, block(0)], vh[h, block(0)])
        s1 = dot_tn(kh[h, block(1)], vh[h, block(1)])
        inner[0, h] = s0
        put_own(0, h, s0 + s1)

    def local(h):
        for b in range(2):
            q0, q1 = qh[h, first(b, 0)], qh[h, first(b, 1)]
            k0, k1 = kh[h, first(b, 0)], kh[h, first(b, 1)]
            v0, v1 = vh[h, first(b, 0)], vh[h, first(b, 1)]
            t00 = causal(dot_nt(q0, k0)).astype(BF16)
            t10 = dot_nt(q1, k0).astype(BF16)
            t11 = causal(dot_nt(q1, k1)).astype(BF16)
            sc[h, b, 0] = t00
            sc[h, b, 1] = t10
            sc[h, b, 2] = t11
            att[h, first(b, 0)] = dot_nn(t00, v0)
            att[h, first(b, 1)] = dot_nn(t10, v0) + dot_nn(t11, v1)

    def attend(h):
        base = get_result(0, h)
        states = (base.astype(BF16), (base + inner[0, h]).astype(BF16))
        gain = gain_ref[h]
        for b in range(2):
            prior[h, b] = states[b]
            for i in range(2):
                rows = first(b, i)
                value = att[h, rows] + dot_nn(qh[h, rows], states[b])
                att[h, rows] = value
                scaled = dyh[h, rows].astype(F32) * gain
                squares[rows] = squares[rows] + value * value
                dots[rows] = dots[rows] + scaled * value

    def row_factors():
        for b in range(2):
            for i in range(2):
                rows = first(b, i)
                mean_sq = jnp.sum(squares[rows], axis=1, keepdims=True) * (1.0 / D)
                mean_dot = jnp.sum(dots[rows], axis=1, keepdims=True) * (1.0 / D)
                inverse = lax.rsqrt(mean_sq + EPSILON)
                mix = inverse * inverse * (inverse * mean_dot)
                inv_rows[rows] = jnp.broadcast_to(inverse, (HALF, HD))
                mix_rows[rows] = jnp.broadcast_to(mix, (HALF, HD))

    def grad_state(h):
        gain = gain_ref[h]
        parts = []
        for b in range(2):
            rows = block(b)
            scaled = dyh[h, rows].astype(F32) * gain
            grad = (inv_rows[rows] * scaled - mix_rows[rows] * att[h, rows]).astype(BF16)
            ga[h, rows] = grad
            parts.append(dot_tn(qh[h, rows], grad))
        inner[1, h] = parts[1]
        put_own(1, h, parts[0] + parts[1])

    def normed(h):
        gain = gain_ref[h]
        no_ref[:, columns(h)] = (att[h] * inv_rows[...] * gain).astype(BF16)

    def backward(h):
        normed(h)
        for b in range(2):
            q0, q1 = qh[h, first(b, 0)], qh[h, first(b, 1)]
            k0, k1 = kh[h, first(b, 0)], kh[h, first(b, 1)]
            v0, v1 = vh[h, first(b, 0)], vh[h, first(b, 1)]
            g0, g1 = ga[h, first(b, 0)], ga[h, first(b, 1)]
            p = prior[h, b]
            s00 = causal(dot_nt(g0, v0)).astype(BF16)
            s10 = dot_nt(g1, v0).astype(BF16)
            s11 = causal(dot_nt(g1, v1)).astype(BF16)
            gq_ref[first(b, 0), columns(h)] = (dot_nt(g0, p) + dot_nn(s00, k0)).astype(BF16)
            gq_ref[first(b, 1), columns(h)] = (dot_nt(g1, p) + dot_nn(s10, k0) + dot_nn(s11, k1)).astype(BF16)
            lk[h, first(b, 0)] = dot_tn(s00, q0) + dot_tn(s10, q1)
            lk[h, first(b, 1)] = dot_tn(s11, q1)
            lv[h, first(b, 0)] = dot_tn(sc[h, b, 0], g0) + dot_tn(sc[h, b, 1], g1)
            lv[h, first(b, 1)] = dot_tn(sc[h, b, 2], g1)

    def finish(h):
        base = get_result(1, h)
        states = ((base + inner[1, h]).astype(BF16), base.astype(BF16))
        for b in range(2):
            rows = block(b)
            gk_ref[rows, columns(h)] = (lk[h, rows] + dot_nt(vh[h, rows], states[b])).astype(BF16)
            gv_ref[rows, columns(h)] = (lv[h, rows] + dot_nn(kh[h, rows], states[b])).astype(BF16)

    barrier = pltpu.get_barrier_semaphore()

    for to in shard_peers:
        pl.semaphore_signal(barrier, inc=1, device_id=(grp, to), device_id_type=MESH)
    for to in group_peers:
        pl.semaphore_signal(barrier, inc=1, device_id=(to, seq), device_id_type=MESH)
    start_loads((0, 1))
    start_loads((2, 3))
    gain_copy = pltpu.make_async_copy(gain_hbm, gain_ref, gain_sem)
    gain_copy.start()

    for c in range(CHUNKS):
        each(c * HPC, (c + 1) * HPC, key_state)
        if c == 0:
            pl.semaphore_wait(barrier, shards - 1 + groups - 1)
        send_parts(0, c)

    def wait_q(h):
        load(2, h).wait()
        load(3, h).wait()

    each(0, H, wait_q)
    gain_copy.wait()
    squares[...] = jnp.zeros_like(squares)
    dots[...] = jnp.zeros_like(dots)
    each(0, 6, local)
    scan_parts(0, 0)
    each(6, 7, local)
    scan_parts(0, 1)
    each(7, 8, local)
    scan_parts(0, 2)
    return_parts(0, 0)
    scan_parts(0, 3)
    return_parts(0, 1)
    return_parts(0, 2)
    return_parts(0, 3)
    for c in range(CHUNKS):
        wait_result(0, c)
        each(c * HPC, (c + 1) * HPC, attend)
    row_factors()
    for c in range(CHUNKS):
        each(c * HPC, (c + 1) * HPC, grad_state)
        send_parts(1, c)
    each(0, 3, backward)
    scan_parts(1, 0)
    each(3, 4, backward)
    scan_parts(1, 1)
    each(4, 5, backward)
    scan_parts(1, 2)
    return_parts(1, 0)
    each(5, 6, backward)
    scan_parts(1, 3)
    return_parts(1, 1)
    return_parts(1, 2)
    return_parts(1, 3)
    each(6, 8, backward)
    for c in range(CHUNKS):
        wait_result(1, c)
        each(c * HPC, (c + 1) * HPC, finish)
    for w in range(2):
        for c in range(CHUNKS):
            wait_sends(w, c)


def body(groups, shards, queries, key_rows, value_rows, norm_gain, cotangent):
    sub = HPC * HD // shards
    whole = pltpu.VMEM((TOK, D), BF16)
    anywhere = pl.BlockSpec(memory_space=pltpu.HBM)
    heads = lambda kind: pltpu.VMEM((H, TOK, HD), kind)
    parts = pltpu.VMEM((2, CHUNKS, shards, sub, HD), F32)
    return tuple(write_out(pl.pallas_call(
        functools.partial(kernel, groups, shards),
        out_shape=(whole,) * 4,
        in_specs=[anywhere] * 5,
        out_specs=(pl.BlockSpec(memory_space=pltpu.VMEM),) * 4,
        scratch_shapes=[
            heads(BF16), heads(BF16), heads(BF16), heads(BF16),
            pltpu.VMEM((H, 2, 3, HALF, HALF), BF16),
            heads(F32), heads(BF16), heads(F32), heads(F32),
            parts, parts, parts,
            pltpu.VMEM((2, CHUNKS, sub, HD), F32),
            pltpu.VMEM((2, CHUNKS, groups, sub, HD), F32),
            parts,
            pltpu.VMEM((2, H, HD, HD), F32),
            pltpu.VMEM((H, 2, HD, HD), BF16),
            pltpu.VMEM((TOK, HD), F32), pltpu.VMEM((TOK, HD), F32),
            pltpu.VMEM((TOK, HD), F32), pltpu.VMEM((TOK, HD), F32),
            pltpu.VMEM((H, 1, HD), F32),
            pltpu.SemaphoreType.DMA((4, H)),
            pltpu.SemaphoreType.DMA,
            pltpu.SemaphoreType.DMA((2, CHUNKS, 3)),
            pltpu.SemaphoreType.DMA((2, CHUNKS, 3)),
        ],
        compiler_params=pltpu.CompilerParams(
            collective_id=0, has_side_effects=True, vmem_limit_bytes=50 * 1024 * 1024
        ),
        name="attention",
    )(queries, key_rows, value_rows, norm_gain.reshape(H, 1, HD), cotangent)))


def write_kernel(a, b, c, d, ao, bo, co, do, sems):
    copies = []
    for i, (src, dst) in enumerate(((a, ao), (b, bo), (c, co), (d, do))):
        for j in range(PIECES):
            rows = pl.ds(j * (TOK // PIECES), TOK // PIECES)
            copies.append(pltpu.make_async_copy(src.at[rows], dst.at[rows], sems.at[i, j]))
    for copy in copies:
        copy.start()
    for copy in copies:
        copy.wait()


def write_out(arrays):
    whole = jax.ShapeDtypeStruct((TOK, D), BF16)
    return pl.pallas_call(
        write_kernel,
        out_shape=(whole,) * 4,
        in_specs=[pl.BlockSpec(memory_space=pl.ANY)] * 4,
        out_specs=(pl.BlockSpec(memory_space=pltpu.HBM),) * 4,
        scratch_shapes=[pltpu.SemaphoreType.DMA((4, PIECES))],
        compiler_params=pltpu.CompilerParams(vmem_limit_bytes=1024 * 1024),
        name="write_out",
    )(*(pltpu.with_memory_space_constraint(a, pltpu.VMEM) for a in arrays))


def solution(mesh):
    rows = P(("grp", "seq"), None)
    return jax.shard_map(
        functools.partial(body, mesh.shape["grp"], mesh.shape["seq"]),
        mesh=mesh,
        in_specs=(rows, rows, rows, P(), rows),
        out_specs=(rows,) * 4,
        check_vma=False,
    )
```

```python
import functools

import jax
import jax.numpy as jnp
from jax import lax
from jax.experimental import pallas as pl
from jax.experimental.pallas import tpu as pltpu
from jax.sharding import PartitionSpec as P

H = 8
HD = 128
BLOCK = 512
HALF = 256
D = H * HD
TOK = 1024
BOUNDS = (0, 1, 3, 5, 7, 8)
CHUNKS = len(BOUNDS) - 1
PIECES = 2
FORWARD = (
    ("h", 3), ("s", 0), ("h", 1), ("s", 1), ("h", 1), ("s", 2), ("r", 0), ("s", 3), ("s", 4), ("r", 1), ("h", 1), ("r", 2), ("r", 3), ("r", 4), ("h", 2),
)
BACKWARD = (
    ("h", 2), ("s", 0), ("h", 1), ("s", 1), ("h", 1), ("s", 2), ("r", 0), ("s", 3), ("s", 4), ("r", 1), ("h", 1), ("r", 2), ("r", 3), ("r", 4), ("h", 3),
)
EPSILON = 1e-06
F32 = jnp.float32
BF16 = jnp.bfloat16
MESH = pl.DeviceIdType.MESH


def dot_nn(a, b):
    return lax.dot_general(a, b, (((1,), (0,)), ((), ())), preferred_element_type=F32)


def dot_nt(a, b):
    return lax.dot_general(a, b, (((1,), (1,)), ((), ())), preferred_element_type=F32)


def dot_tn(a, b):
    return lax.dot_general(a, b, (((0,), (0,)), ((), ())), preferred_element_type=F32)


def causal(tile):
    rows = lax.broadcasted_iota(jnp.int32, tile.shape, 0)
    cols = lax.broadcasted_iota(jnp.int32, tile.shape, 1)
    return jnp.where(rows >= cols, tile, 0.0)


def causal_t(tile):
    rows = lax.broadcasted_iota(jnp.int32, tile.shape, 0)
    cols = lax.broadcasted_iota(jnp.int32, tile.shape, 1)
    return jnp.where(cols >= rows, tile, 0.0)


def kernel(
    groups, shards,
    q_hbm, k_hbm, v_hbm, gain_hbm, dy_hbm,
    no_ref, gq_ref, gk_ref, gv_ref,
    qh, kh, vh, dyh, qt, sc, att, ga, lk, lv,
    own, arrived, before, total, peers, result, inner, prior,
    squares, dots, inv_rows, mix_rows,
    gain_ref, in_sem, gain_sem, send_sem, recv_sem,
):
    grp = lax.axis_index("grp")
    seq = lax.axis_index("seq")
    sub = HD // shards

    def span(c):
        return pl.ds(BOUNDS[c], BOUNDS[c + 1] - BOUNDS[c])

    def ring(step):
        return min(step, 4 - step)

    offsets = [(dz, dx) for dz in range(shards // 4) for dx in range(4) if dz or dx]
    offsets.sort(key=lambda o: -ring(o[0]) - ring(o[1]))
    shard_peers = [
        lax.rem(seq // 4 + dz, shards // 4) * 4 + lax.rem(seq % 4 + dx, 4) for dz, dx in offsets
    ]
    offsets = [(dy, dc) for dy in range(groups // 2) for dc in range(2) if dy or dc]
    offsets.sort(key=lambda o: -ring(o[0]) * 2 - o[1])
    group_peers = [
        lax.rem(grp // 2 + dy, groups // 2) * 2 + lax.rem(grp % 2 + dc, 2) for dy, dc in offsets
    ]

    def columns(h):
        return pl.ds(pl.multiple_of(h * HD, HD), HD)

    def load(i, h):
        src = (k_hbm, v_hbm, q_hbm, dy_hbm)[i]
        dst = (kh, vh, qh, dyh)[i]
        return pltpu.make_async_copy(src.at[:, columns(h)], dst.at[h], in_sem.at[i, h])

    def each(lo, hi, fn):
        def step(h, carry):
            fn(h)
            return carry
        lax.fori_loop(lo, hi, step, 0)

    def start_loads(arrays):
        def one(h):
            for i in arrays:
                load(i, h).start()
        each(0, H, one)

    def sent(w, c, phase, src, dst, device):
        return pltpu.make_async_remote_copy(
            src, dst, send_sem.at[w, c, phase], recv_sem.at[w, c, phase],
            device_id=device, device_id_type=MESH,
        )

    def all_of(w, c, phase):
        ref, count = ((own, shards), (peers, groups), (before, shards))[phase]
        part = ref.at[w, span(c), pl.ds(0, count - 1)]
        return sent(w, c, phase, part, part, (grp, seq))

    def send_parts(w, c):
        for to in shard_peers:
            sent(w, c, 0, own.at[w, span(c), to], arrived.at[w, span(c), seq], (grp, to)).start()
        arrived[w, span(c), seq] = own[w, span(c), seq]

    def scan_parts(w, c):
        all_of(w, c, 0).wait_recv()
        order = range(shards) if w == 0 else range(shards - 1, -1, -1)
        parts = [arrived[w, span(c), t] for t in order]
        sums = parts
        while len(sums) > 1:
            sums = [sums[i] + sums[i + 1] for i in range(0, len(sums), 2)]
        total[w, span(c)] = sums[0]
        for to in group_peers:
            sent(w, c, 1, total.at[w, span(c)], peers.at[w, span(c), grp], (to, seq)).start()
        peers[w, span(c), grp] = sums[0]
        running = jnp.zeros_like(sums[0])
        for t, part in zip(order, parts):
            before[w, span(c), t] = running
            running = running + part

    def return_parts(w, c):
        all_of(w, c, 1).wait_recv()
        base = jnp.zeros((BOUNDS[c + 1] - BOUNDS[c], sub, HD), F32)
        for g in range(groups):
            inside = g < grp if w == 0 else g > grp
            base = base + jnp.where(inside, peers[w, span(c), g], 0.0)
        for t in range(shards):
            before[w, span(c), t] = before[w, span(c), t] + base
        for to in shard_peers:
            sent(w, c, 2, before.at[w, span(c), to], result.at[w, span(c), seq], (grp, to)).start()
        result[w, span(c), seq] = before[w, span(c), seq]

    def wait_result(w, c):
        all_of(w, c, 2).wait_recv()

    def wait_sends(w, c):
        for phase in range(3):
            all_of(w, c, phase).wait_send()

    def put_own(w, h, value):
        own[w, h] = value.reshape(shards, sub, HD)

    def get_result(w, h):
        return result[w, h].reshape(HD, HD)

    def first(b, i):
        return pl.ds(b * BLOCK + i * HALF, HALF)

    def block(b):
        return pl.ds(b * BLOCK, BLOCK)

    def key_state(h):
        load(0, h).wait()
        load(1, h).wait()
        s0 = dot_tn(kh[h, block(0)], vh[h, block(0)])
        s1 = dot_tn(kh[h, block(1)], vh[h, block(1)])
        inner[0, h] = s0
        put_own(0, h, s0 + s1)

    def local(h):
        for b in range(2):
            q0, q1 = qh[h, first(b, 0)], qh[h, first(b, 1)]
            k0, k1 = kh[h, first(b, 0)], kh[h, first(b, 1)]
            v0, v1 = vh[h, first(b, 0)], vh[h, first(b, 1)]
            t00 = causal(dot_nt(q0, k0)).astype(BF16)
            t10 = dot_nt(q1, k0).astype(BF16)
            t11 = causal(dot_nt(q1, k1)).astype(BF16)
            sc[h, b, 0] = causal_t(dot_nt(k0, q0)).astype(BF16)
            sc[h, b, 1] = dot_nt(k0, q1).astype(BF16)
            sc[h, b, 2] = causal_t(dot_nt(k1, q1)).astype(BF16)
            qt[h, :, block(b)] = jnp.transpose(qh[h, block(b)])
            att[h, first(b, 0)] = dot_nn(t00, v0)
            att[h, first(b, 1)] = dot_nn(t10, v0) + dot_nn(t11, v1)

    def attend(h):
        base = get_result(0, h)
        states = (base.astype(BF16), (base + inner[0, h]).astype(BF16))
        gain = gain_ref[h]
        for b in range(2):
            prior[h, b] = states[b]
            for i in range(2):
                rows = first(b, i)
                value = att[h, rows] + dot_nn(qh[h, rows], states[b])
                att[h, rows] = value
                scaled = dyh[h, rows].astype(F32) * gain
                squares[rows] = squares[rows] + value * value
                dots[rows] = dots[rows] + scaled * value

    def row_factors():
        for b in range(2):
            for i in range(2):
                rows = first(b, i)
                mean_sq = jnp.sum(squares[rows], axis=1, keepdims=True) * (1.0 / D)
                mean_dot = jnp.sum(dots[rows], axis=1, keepdims=True) * (1.0 / D)
                inverse = lax.rsqrt(mean_sq + EPSILON)
                mix = inverse * inverse * (inverse * mean_dot)
                inv_rows[rows] = jnp.broadcast_to(inverse, (HALF, HD))
                mix_rows[rows] = jnp.broadcast_to(mix, (HALF, HD))

    def grad_state(h):
        gain = gain_ref[h]
        parts = []
        for b in range(2):
            rows = block(b)
            scaled = dyh[h, rows].astype(F32) * gain
            grad = (inv_rows[rows] * scaled - mix_rows[rows] * att[h, rows]).astype(BF16)
            ga[h, rows] = grad
            parts.append(dot_nn(qt[h, :, rows], grad))
        inner[1, h] = parts[1]
        put_own(1, h, parts[0] + parts[1])

    def normed(h):
        gain = gain_ref[h]
        no_ref[:, columns(h)] = (att[h] * inv_rows[...] * gain).astype(BF16)

    def backward(h):
        normed(h)
        for b in range(2):
            q0, q1 = qt[h, :, first(b, 0)], qt[h, :, first(b, 1)]
            k0, k1 = kh[h, first(b, 0)], kh[h, first(b, 1)]
            v0, v1 = vh[h, first(b, 0)], vh[h, first(b, 1)]
            g0, g1 = ga[h, first(b, 0)], ga[h, first(b, 1)]
            p = prior[h, b]
            s00 = causal(dot_nt(g0, v0)).astype(BF16)
            s10 = dot_nt(g1, v0).astype(BF16)
            s11 = causal(dot_nt(g1, v1)).astype(BF16)
            gq_ref[first(b, 0), columns(h)] = (dot_nt(g0, p) + dot_nn(s00, k0)).astype(BF16)
            gq_ref[first(b, 1), columns(h)] = (dot_nt(g1, p) + dot_nn(s10, k0) + dot_nn(s11, k1)).astype(BF16)
            lk[h, first(b, 0)] = jnp.transpose(dot_nn(q0, s00) + dot_nn(q1, s10))
            lk[h, first(b, 1)] = jnp.transpose(dot_nn(q1, s11))
            lv[h, first(b, 0)] = dot_nn(sc[h, b, 0], g0) + dot_nn(sc[h, b, 1], g1)
            lv[h, first(b, 1)] = dot_nn(sc[h, b, 2], g1)

    def finish(h):
        base = get_result(1, h)
        states = ((base + inner[1, h]).astype(BF16), base.astype(BF16))
        for b in range(2):
            rows = block(b)
            gk_ref[rows, columns(h)] = (lk[h, rows] + dot_nt(vh[h, rows], states[b])).astype(BF16)
            gv_ref[rows, columns(h)] = (lv[h, rows] + dot_nn(kh[h, rows], states[b])).astype(BF16)

    barrier = pltpu.get_barrier_semaphore()

    for to in shard_peers:
        pl.semaphore_signal(barrier, inc=1, device_id=(grp, to), device_id_type=MESH)
    for to in group_peers:
        pl.semaphore_signal(barrier, inc=1, device_id=(to, seq), device_id_type=MESH)
    start_loads((0, 1))
    for c in range(CHUNKS):
        each(BOUNDS[c], BOUNDS[c + 1], key_state)
        if c == 0:
            pl.semaphore_wait(barrier, shards - 1 + groups - 1)
        send_parts(0, c)
        if c == 0:
            start_loads((2, 3))
            gain_copy = pltpu.make_async_copy(gain_hbm, gain_ref, gain_sem)
            gain_copy.start()

    def wait_q(h):
        load(2, h).wait()
        load(3, h).wait()

    each(0, H, wait_q)
    gain_copy.wait()
    squares[...] = jnp.zeros_like(squares)
    dots[...] = jnp.zeros_like(dots)
    def run(plan, w, work):
        done = 0
        for kind, n in plan:
            if kind == "s":
                scan_parts(w, n)
            elif kind == "r":
                return_parts(w, n)
            else:
                each(done, done + n, work)
                done += n

    run(FORWARD, 0, local)
    for c in range(CHUNKS):
        wait_result(0, c)
        each(BOUNDS[c], BOUNDS[c + 1], attend)
    row_factors()
    for c in range(CHUNKS):
        each(BOUNDS[c], BOUNDS[c + 1], grad_state)
        send_parts(1, c)
    run(BACKWARD, 1, backward)
    for c in range(CHUNKS):
        wait_result(1, c)
        each(BOUNDS[c], BOUNDS[c + 1], finish)
    for w in range(2):
        for c in range(CHUNKS):
            wait_sends(w, c)


def body(groups, shards, queries, key_rows, value_rows, norm_gain, cotangent):
    sub = HD // shards
    whole = pltpu.VMEM((TOK, D), BF16)
    anywhere = pl.BlockSpec(memory_space=pltpu.HBM)
    heads = lambda kind: pltpu.VMEM((H, TOK, HD), kind)
    parts = pltpu.VMEM((2, H, shards, sub, HD), F32)
    return tuple(write_out(pl.pallas_call(
        functools.partial(kernel, groups, shards),
        out_shape=(whole,) * 4,
        in_specs=[anywhere] * 5,
        out_specs=(pl.BlockSpec(memory_space=pltpu.VMEM),) * 4,
        scratch_shapes=[
            heads(BF16), heads(BF16), heads(BF16), heads(BF16),
            pltpu.VMEM((H, HD, TOK), BF16),
            pltpu.VMEM((H, 2, 3, HALF, HALF), BF16),
            heads(F32), heads(BF16), heads(F32), heads(F32),
            parts, parts, parts,
            pltpu.VMEM((2, H, sub, HD), F32),
            pltpu.VMEM((2, H, groups, sub, HD), F32),
            parts,
            pltpu.VMEM((2, H, HD, HD), F32),
            pltpu.VMEM((H, 2, HD, HD), BF16),
            pltpu.VMEM((TOK, HD), F32), pltpu.VMEM((TOK, HD), F32),
            pltpu.VMEM((TOK, HD), F32), pltpu.VMEM((TOK, HD), F32),
            pltpu.VMEM((H, 1, HD), F32),
            pltpu.SemaphoreType.DMA((4, H)),
            pltpu.SemaphoreType.DMA,
            pltpu.SemaphoreType.DMA((2, CHUNKS, 3)),
            pltpu.SemaphoreType.DMA((2, CHUNKS, 3)),
        ],
        compiler_params=pltpu.CompilerParams(
            collective_id=0, has_side_effects=True, vmem_limit_bytes=50 * 1024 * 1024
        ),
        name="attention",
    )(queries, key_rows, value_rows, norm_gain.reshape(H, 1, HD), cotangent)))


def write_kernel(a, b, c, d, ao, bo, co, do, sems):
    copies = []
    for i, (src, dst) in enumerate(((a, ao), (b, bo), (c, co), (d, do))):
        for j in range(PIECES):
            rows = pl.ds(j * (TOK // PIECES), TOK // PIECES)
            copies.append(pltpu.make_async_copy(src.at[rows], dst.at[rows], sems.at[i, j]))
    for copy in copies:
        copy.start()
    for copy in copies:
        copy.wait()


def write_out(arrays):
    whole = jax.ShapeDtypeStruct((TOK, D), BF16)
    return pl.pallas_call(
        write_kernel,
        out_shape=(whole,) * 4,
        in_specs=[pl.BlockSpec(memory_space=pl.ANY)] * 4,
        out_specs=(pl.BlockSpec(memory_space=pltpu.HBM),) * 4,
        scratch_shapes=[pltpu.SemaphoreType.DMA((4, PIECES))],
        compiler_params=pltpu.CompilerParams(vmem_limit_bytes=1024 * 1024),
        name="write_out",
    )(*(pltpu.with_memory_space_constraint(a, pltpu.VMEM) for a in arrays))


def solution(mesh):
    rows = P(("grp", "seq"), None)
    return jax.shard_map(
        functools.partial(body, mesh.shape["grp"], mesh.shape["seq"]),
        mesh=mesh,
        in_specs=(rows, rows, rows, P(), rows),
        out_specs=(rows,) * 4,
        check_vma=False,
    )
```

```python
import functools

import jax
import jax.numpy as jnp
from jax import lax
from jax.experimental import pallas as pl
from jax.experimental.pallas import tpu as pltpu
from jax.sharding import PartitionSpec as P

H = 8
HD = 128
BLOCK = 512
HALF = 256
D = H * HD
TOK = 1024
BOUNDS = (0, 1, 3, 5, 7, 8)
CHUNKS = len(BOUNDS) - 1
PIECES = 2
FORWARD = (
    ("h", 3), ("s", 0), ("h", 1), ("s", 1), ("h", 1), ("s", 2), ("r", 0), ("s", 3), ("s", 4), ("r", 1), ("h", 1), ("r", 2), ("r", 3), ("r", 4), ("h", 2),
)
BACKWARD = (
    ("h", 2), ("s", 0), ("h", 1), ("s", 1), ("h", 1), ("s", 2), ("r", 0), ("s", 3), ("s", 4), ("r", 1), ("h", 1), ("r", 2), ("r", 3), ("r", 4), ("h", 3),
)
EPSILON = 1e-06
F32 = jnp.float32
BF16 = jnp.bfloat16
MESH = pl.DeviceIdType.MESH


def dot_nn(a, b):
    return lax.dot_general(a, b, (((1,), (0,)), ((), ())), preferred_element_type=F32)


def dot_nt(a, b):
    return lax.dot_general(a, b, (((1,), (1,)), ((), ())), preferred_element_type=F32)


def dot_tn(a, b):
    return lax.dot_general(a, b, (((0,), (0,)), ((), ())), preferred_element_type=F32)


def causal(tile):
    rows = lax.broadcasted_iota(jnp.int32, tile.shape, 0)
    cols = lax.broadcasted_iota(jnp.int32, tile.shape, 1)
    return jnp.where(rows >= cols, tile, 0.0)


def causal_t(tile):
    rows = lax.broadcasted_iota(jnp.int32, tile.shape, 0)
    cols = lax.broadcasted_iota(jnp.int32, tile.shape, 1)
    return jnp.where(cols >= rows, tile, 0.0)


def kernel(
    groups, shards,
    q_hbm, k_hbm, v_hbm, gain_hbm, dy_hbm,
    no_ref, gq_ref, gk_ref, gv_ref,
    qh, kh, vh, dyh, qt, sc, att, ga, lk, lv,
    own, arrived, before, total, peers, result, inner, prior,
    squares, dots, inv_rows, mix_rows,
    gain_ref, in_sem, gain_sem, send_sem, recv_sem,
):
    grp = lax.axis_index("grp")
    seq = lax.axis_index("seq")
    sub = HD // shards

    def span(c):
        return pl.ds(BOUNDS[c], BOUNDS[c + 1] - BOUNDS[c])

    def ring(step):
        return min(step, 4 - step)

    offsets = [(dz, dx) for dz in range(shards // 4) for dx in range(4) if dz or dx]
    offsets.sort(key=lambda o: -ring(o[0]) - ring(o[1]))
    shard_peers = [
        lax.rem(seq // 4 + dz, shards // 4) * 4 + lax.rem(seq % 4 + dx, 4) for dz, dx in offsets
    ]
    offsets = [(dy, dc) for dy in range(groups // 2) for dc in range(2) if dy or dc]
    offsets.sort(key=lambda o: -ring(o[0]) * 2 - o[1])
    group_peers = [
        lax.rem(grp // 2 + dy, groups // 2) * 2 + lax.rem(grp % 2 + dc, 2) for dy, dc in offsets
    ]

    def columns(h):
        return pl.ds(pl.multiple_of(h * HD, HD), HD)

    def load(i, h):
        src = (k_hbm, v_hbm, q_hbm, dy_hbm)[i]
        dst = (kh, vh, qh, dyh)[i]
        return pltpu.make_async_copy(src.at[:, columns(h)], dst.at[h], in_sem.at[i, h])

    def each(lo, hi, fn):
        if hi - lo == 1:
            fn(lo)
            return

        def step(h, carry):
            fn(h)
            return carry
        lax.fori_loop(lo, hi, step, 0)

    def start_loads(arrays):
        def one(h):
            for i in arrays:
                load(i, h).start()
        each(0, H, one)

    def sent(w, c, phase, src, dst, device):
        return pltpu.make_async_remote_copy(
            src, dst, send_sem.at[w, c, phase], recv_sem.at[w, c, phase],
            device_id=device, device_id_type=MESH,
        )

    def all_of(w, c, phase):
        ref, count = ((own, shards), (peers, groups), (before, shards))[phase]
        part = ref.at[w, span(c), pl.ds(0, count - 1)]
        return sent(w, c, phase, part, part, (grp, seq))

    def send_parts(w, c):
        for to in shard_peers:
            sent(w, c, 0, own.at[w, span(c), to], arrived.at[w, span(c), seq], (grp, to)).start()
        arrived[w, span(c), seq] = own[w, span(c), seq]

    def scan_parts(w, c):
        all_of(w, c, 0).wait_recv()
        order = range(shards) if w == 0 else range(shards - 1, -1, -1)
        parts = [arrived[w, span(c), t] for t in order]
        sums = parts
        while len(sums) > 1:
            sums = [sums[i] + sums[i + 1] for i in range(0, len(sums), 2)]
        total[w, span(c)] = sums[0]
        for to in group_peers:
            sent(w, c, 1, total.at[w, span(c)], peers.at[w, span(c), grp], (to, seq)).start()
        peers[w, span(c), grp] = sums[0]
        running = jnp.zeros_like(sums[0])
        for t, part in zip(order, parts):
            before[w, span(c), t] = running
            running = running + part

    def return_parts(w, c):
        all_of(w, c, 1).wait_recv()
        base = jnp.zeros((BOUNDS[c + 1] - BOUNDS[c], sub, HD), F32)
        for g in range(groups):
            inside = g < grp if w == 0 else g > grp
            base = base + jnp.where(inside, peers[w, span(c), g], 0.0)
        for t in range(shards):
            before[w, span(c), t] = before[w, span(c), t] + base
        for to in shard_peers:
            sent(w, c, 2, before.at[w, span(c), to], result.at[w, span(c), seq], (grp, to)).start()
        result[w, span(c), seq] = before[w, span(c), seq]

    def wait_result(w, c):
        all_of(w, c, 2).wait_recv()

    def wait_sends(w, c):
        for phase in range(3):
            all_of(w, c, phase).wait_send()

    def put_own(w, h, value):
        own[w, h] = value.reshape(shards, sub, HD)

    def get_result(w, h):
        return result[w, h].reshape(HD, HD)

    def first(b, i):
        return pl.ds(b * BLOCK + i * HALF, HALF)

    def block(b):
        return pl.ds(b * BLOCK, BLOCK)

    def key_state(h):
        load(0, h).wait()
        load(1, h).wait()
        s0 = dot_tn(kh[h, block(0)], vh[h, block(0)])
        s1 = dot_tn(kh[h, block(1)], vh[h, block(1)])
        inner[0, h] = s0
        put_own(0, h, s0 + s1)

    def local(h):
        load(2, h).wait()
        for b in range(2):
            q0, q1 = qh[h, first(b, 0)], qh[h, first(b, 1)]
            k0, k1 = kh[h, first(b, 0)], kh[h, first(b, 1)]
            v0, v1 = vh[h, first(b, 0)], vh[h, first(b, 1)]
            t00 = causal(dot_nt(q0, k0)).astype(BF16)
            t10 = dot_nt(q1, k0).astype(BF16)
            t11 = causal(dot_nt(q1, k1)).astype(BF16)
            sc[h, b, 0] = causal_t(dot_nt(k0, q0)).astype(BF16)
            sc[h, b, 1] = dot_nt(k0, q1).astype(BF16)
            sc[h, b, 2] = causal_t(dot_nt(k1, q1)).astype(BF16)
            qt[h, :, block(b)] = jnp.transpose(qh[h, block(b)])
            att[h, first(b, 0)] = dot_nn(t00, v0)
            att[h, first(b, 1)] = dot_nn(t10, v0) + dot_nn(t11, v1)

    def attend(h):
        base = get_result(0, h)
        states = (base.astype(BF16), (base + inner[0, h]).astype(BF16))
        gain = gain_ref[h]
        for b in range(2):
            prior[h, b] = states[b]
            for i in range(2):
                rows = first(b, i)
                value = att[h, rows] + dot_nn(qh[h, rows], states[b])
                att[h, rows] = value
                scaled = dyh[h, rows].astype(F32) * gain
                squares[rows] = squares[rows] + value * value
                dots[rows] = dots[rows] + scaled * value

    def row_factors():
        for b in range(2):
            for i in range(2):
                rows = first(b, i)
                mean_sq = jnp.sum(squares[rows], axis=1, keepdims=True) * (1.0 / D)
                mean_dot = jnp.sum(dots[rows], axis=1, keepdims=True) * (1.0 / D)
                inverse = lax.rsqrt(mean_sq + EPSILON)
                mix = inverse * inverse * (inverse * mean_dot)
                inv_rows[rows] = jnp.broadcast_to(inverse, (HALF, HD))
                mix_rows[rows] = jnp.broadcast_to(mix, (HALF, HD))

    def grad_state(h):
        gain = gain_ref[h]
        parts = []
        for b in range(2):
            rows = block(b)
            scaled = dyh[h, rows].astype(F32) * gain
            grad = (inv_rows[rows] * scaled - mix_rows[rows] * att[h, rows]).astype(BF16)
            ga[h, rows] = grad
            parts.append(dot_nn(qt[h, :, rows], grad))
        inner[1, h] = parts[1]
        put_own(1, h, parts[0] + parts[1])

    def normed(h):
        gain = gain_ref[h]
        no_ref[:, columns(h)] = (att[h] * inv_rows[...] * gain).astype(BF16)

    def backward(h):
        normed(h)
        for b in range(2):
            q0, q1 = qt[h, :, first(b, 0)], qt[h, :, first(b, 1)]
            k0, k1 = kh[h, first(b, 0)], kh[h, first(b, 1)]
            v0, v1 = vh[h, first(b, 0)], vh[h, first(b, 1)]
            g0, g1 = ga[h, first(b, 0)], ga[h, first(b, 1)]
            p = prior[h, b]
            s00 = causal(dot_nt(g0, v0)).astype(BF16)
            s10 = dot_nt(g1, v0).astype(BF16)
            s11 = causal(dot_nt(g1, v1)).astype(BF16)
            gq_ref[first(b, 0), columns(h)] = (dot_nt(g0, p) + dot_nn(s00, k0)).astype(BF16)
            gq_ref[first(b, 1), columns(h)] = (dot_nt(g1, p) + dot_nn(s10, k0) + dot_nn(s11, k1)).astype(BF16)
            lk[h, first(b, 0)] = jnp.transpose(dot_nn(q0, s00) + dot_nn(q1, s10))
            lk[h, first(b, 1)] = jnp.transpose(dot_nn(q1, s11))
            lv[h, first(b, 0)] = dot_nn(sc[h, b, 0], g0) + dot_nn(sc[h, b, 1], g1)
            lv[h, first(b, 1)] = dot_nn(sc[h, b, 2], g1)

    def finish(h):
        base = get_result(1, h)
        states = ((base + inner[1, h]).astype(BF16), base.astype(BF16))
        for b in range(2):
            rows = block(b)
            gk_ref[rows, columns(h)] = (lk[h, rows] + dot_nt(vh[h, rows], states[b])).astype(BF16)
            gv_ref[rows, columns(h)] = (lv[h, rows] + dot_nn(kh[h, rows], states[b])).astype(BF16)

    barrier = pltpu.get_barrier_semaphore()

    for to in shard_peers:
        pl.semaphore_signal(barrier, inc=1, device_id=(grp, to), device_id_type=MESH)
    for to in group_peers:
        pl.semaphore_signal(barrier, inc=1, device_id=(to, seq), device_id_type=MESH)
    start_loads((0, 1))
    for c in range(CHUNKS):
        each(BOUNDS[c], BOUNDS[c + 1], key_state)
        if c == 0:
            pl.semaphore_wait(barrier, shards - 1 + groups - 1)
        send_parts(0, c)
        if c == 0:
            start_loads((2, 3))
            gain_copy = pltpu.make_async_copy(gain_hbm, gain_ref, gain_sem)
            gain_copy.start()

    squares[...] = jnp.zeros_like(squares)
    dots[...] = jnp.zeros_like(dots)
    def run(plan, w, work):
        done = 0
        for kind, n in plan:
            if kind == "s":
                scan_parts(w, n)
            elif kind == "r":
                return_parts(w, n)
            else:
                each(done, done + n, work)
                done += n

    run(FORWARD, 0, local)
    each(0, H, lambda h: load(3, h).wait())
    gain_copy.wait()
    for c in range(CHUNKS):
        wait_result(0, c)
        each(BOUNDS[c], BOUNDS[c + 1], attend)
    row_factors()
    for c in range(CHUNKS):
        each(BOUNDS[c], BOUNDS[c + 1], grad_state)
        send_parts(1, c)
    run(BACKWARD, 1, backward)
    for c in range(CHUNKS):
        wait_result(1, c)
        each(BOUNDS[c], BOUNDS[c + 1], finish)
    for w in range(2):
        for c in range(CHUNKS):
            wait_sends(w, c)


def body(groups, shards, queries, key_rows, value_rows, norm_gain, cotangent):
    sub = HD // shards
    whole = pltpu.VMEM((TOK, D), BF16)
    anywhere = pl.BlockSpec(memory_space=pltpu.HBM)
    heads = lambda kind: pltpu.VMEM((H, TOK, HD), kind)
    parts = pltpu.VMEM((2, H, shards, sub, HD), F32)
    return tuple(write_out(pl.pallas_call(
        functools.partial(kernel, groups, shards),
        out_shape=(whole,) * 4,
        in_specs=[anywhere] * 5,
        out_specs=(pl.BlockSpec(memory_space=pltpu.VMEM),) * 4,
        scratch_shapes=[
            heads(BF16), heads(BF16), heads(BF16), heads(BF16),
            pltpu.VMEM((H, HD, TOK), BF16),
            pltpu.VMEM((H, 2, 3, HALF, HALF), BF16),
            heads(F32), heads(BF16), heads(F32), heads(F32),
            parts, parts, parts,
            pltpu.VMEM((2, H, sub, HD), F32),
            pltpu.VMEM((2, H, groups, sub, HD), F32),
            parts,
            pltpu.VMEM((2, H, HD, HD), F32),
            pltpu.VMEM((H, 2, HD, HD), BF16),
            pltpu.VMEM((TOK, HD), F32), pltpu.VMEM((TOK, HD), F32),
            pltpu.VMEM((TOK, HD), F32), pltpu.VMEM((TOK, HD), F32),
            pltpu.VMEM((H, 1, HD), F32),
            pltpu.SemaphoreType.DMA((4, H)),
            pltpu.SemaphoreType.DMA,
            pltpu.SemaphoreType.DMA((2, CHUNKS, 3)),
            pltpu.SemaphoreType.DMA((2, CHUNKS, 3)),
        ],
        compiler_params=pltpu.CompilerParams(
            collective_id=0, has_side_effects=True, vmem_limit_bytes=50 * 1024 * 1024
        ),
        name="attention",
    )(queries, key_rows, value_rows, norm_gain.reshape(H, 1, HD), cotangent)))


def write_kernel(a, b, c, d, ao, bo, co, do, sems):
    copies = []
    for i, (src, dst) in enumerate(((a, ao), (b, bo), (c, co), (d, do))):
        for j in range(PIECES):
            rows = pl.ds(j * (TOK // PIECES), TOK // PIECES)
            copies.append(pltpu.make_async_copy(src.at[rows], dst.at[rows], sems.at[i, j]))
    for copy in copies:
        copy.start()
    for copy in copies:
        copy.wait()


def write_out(arrays):
    whole = jax.ShapeDtypeStruct((TOK, D), BF16)
    return pl.pallas_call(
        write_kernel,
        out_shape=(whole,) * 4,
        in_specs=[pl.BlockSpec(memory_space=pl.ANY)] * 4,
        out_specs=(pl.BlockSpec(memory_space=pltpu.HBM),) * 4,
        scratch_shapes=[pltpu.SemaphoreType.DMA((4, PIECES))],
        compiler_params=pltpu.CompilerParams(vmem_limit_bytes=1024 * 1024),
        name="write_out",
    )(*(pltpu.with_memory_space_constraint(a, pltpu.VMEM) for a in arrays))


def solution(mesh):
    rows = P(("grp", "seq"), None)
    return jax.shard_map(
        functools.partial(body, mesh.shape["grp"], mesh.shape["seq"]),
        mesh=mesh,
        in_specs=(rows, rows, rows, P(), rows),
        out_specs=(rows,) * 4,
        check_vma=False,
    )
```
